256 devices in a mesh: island: 4 (over x_lo, core), fsdp: 64 (over x_hi, y, z).
Axes of the slice: x: 4 (x_hi: 2, x_lo: 2; x = x_hi * 2 + x_lo), y: 4, z: 8, core: 2. Of those that a mesh axis runs over, the one named last changes fastest.
Arguments:
- local_weights: bfloat16 [4, 512, 8192], P('island', 'fsdp'), may hold values from -6 to 6
- base_master: float32 [512, 8192], P('fsdp'), may hold values from -6 to 6
- momentum: float32 [512, 8192], P('fsdp'), may hold values from -4 to 4
Outputs:
- new_master: float32 [512, 8192], P('fsdp')
- new_momentum: float32 [512, 8192], P('fsdp')
- new_base: bfloat16 [512, 8192], replicated
The draws below stay inside these ranges and needn't reach their ends.
All inputs are finite; a program needn't handle non-finite values.
Results may differ from the reference program's by a relative error of at most 0.02.
Values may be sent and summed in bfloat16 or wider, within the bound.
No kernel may reach another device: no remote copies, remote signals or barrier semaphores. Data moves between devices by JAX's collectives and lax.ppermute only.
A program may use at most 64 MiB of HBM per device.

```python
import jax
import jax.numpy as jnp

D = 8192
BLOCK = 128
ROWS = 512
ISLANDS = 4


def shard_levels(own_key, dims, shards, smallest, high):
    level = 1.0
    for axis_at, shards_of in shards:
        steps = jax.random.uniform(jax.random.fold_in(jax.random.fold_in(own_key, 6), axis_at), (shards_of,), jnp.float32, smallest / len(shards), high / len(shards))
        level = level * jnp.repeat(jnp.exp(steps), dims[axis_at] // shards_of).reshape((-1,) + (1,) * (len(dims) - 1 - axis_at))
    return level


def gaussian(stream_key, dims, width, limit, split=(), kind=jnp.bfloat16):
    entries = width * jax.random.normal(stream_key, dims, jnp.float32)
    if split:
        entries = entries * shard_levels(stream_key, dims, split, -0.22, 0.18)
    return jnp.clip(entries, -limit, limit).astype(kind)


def setup_inputs(seed: int = 0) -> dict:
    seeds = jax.random.split(jax.random.key(seed), 4)
    local_weights = gaussian(seeds[0], (ISLANDS, ROWS, D), 1.0, 6.0, ((0, 4), (1, 64)))
    base_master = gaussian(seeds[1], (ROWS, D), 1.0, 6.0, ((0, 64),), jnp.float32)
    momentum = gaussian(seeds[2], (ROWS, D), 0.5, 4.0, ((0, 64),), jnp.float32)
    return dict(local_weights=local_weights, base_master=base_master, momentum=momentum)


epsilon = 1e-6
code_limit = 31.0
momentum_decay = 0.9
outer_rate = 0.7


def decode_group(outer_grad):
    blocks = outer_grad.reshape(outer_grad.shape[0], D // BLOCK, BLOCK)
    largest = jnp.max(jnp.abs(blocks), axis=2, keepdims=True)
    block_scale = (largest + epsilon) / code_limit
    code_values = (blocks / block_scale).astype(jnp.bfloat16)
    return (code_values.astype(jnp.float32) * block_scale).reshape(outer_grad.shape)


def reference(local_weights, base_master, momentum):
    summed = jnp.zeros(base_master.shape, jnp.float32)
    for group_index in range(ISLANDS):
        outer_grad = base_master - local_weights[group_index].astype(jnp.float32)
        summed = summed + decode_group(outer_grad)
    averaged = summed / ISLANDS
    new_momentum = momentum_decay * momentum + averaged
    new_master = base_master - outer_rate * (averaged + momentum_decay * new_momentum)
    return new_master, new_momentum, new_master.astype(jnp.bfloat16)
```

```python
import functools

import jax
import jax.numpy as jnp
from jax import lax
from jax.experimental import pallas as pl
from jax.experimental.pallas import tpu as pltpu
from jax.sharding import PartitionSpec as P

BLOCK = 128

epsilon = 1e-06
code_limit = 31.0
momentum_decay = 0.9
outer_rate = 0.7

AXES = ("island", "fsdp")
RING = 8
HALF = 4096
ROWS = 8


def all_places():
    for x_lo in range(2):
        for core in range(2):
            for x_hi in range(2):
                for y in range(4):
                    for z in range(8):
                        yield x_lo, core, x_hi, y, z


def number(place):
    x_lo, core, x_hi, y, z = place
    return (x_lo * 2 + core) * 64 + (x_hi * 4 + y) * 8 + z


def pairs(target):
    return [(number(p), number(target(*p))) for p in all_places()]


def snake_of(x_hi, y):
    return y if x_hi == 0 else 7 - y


def along_snake(x_lo, core, x_hi, y, z, step):
    at = (snake_of(x_hi, y) + step) % RING
    to_hi, to_y = (0, at) if at < 4 else (1, 7 - at)
    return (x_lo if to_hi == x_hi else 1 - x_lo), core, to_hi, to_y, z


def along_z(x_lo, core, x_hi, y, z, step):
    return x_lo, core, x_hi, y, (z + step) % RING


def first_phase(step):
    return pairs(lambda *p: (along_snake if p[1] == 0 else along_z)(*p, step))


def second_phase(step):
    return pairs(lambda *p: (along_z if p[1] == 0 else along_snake)(*p, step))


OTHER_CORE = pairs(lambda x_lo, core, x_hi, y, z: (x_lo, 1 - core, x_hi, y, z))
OTHER_CHIP = pairs(lambda x_lo, core, x_hi, y, z: (1 - x_lo, core, x_hi, y, z))
OTHER_BOTH = pairs(lambda x_lo, core, x_hi, y, z: (1 - x_lo, 1 - core, x_hi, y, z))


def send(x, to):
    return lax.ppermute(x, AXES, to)


def my_core():
    return lax.rem(lax.axis_index("island"), 2)


def my_z():
    return lax.rem(lax.axis_index("fsdp"), RING)


def my_snake():
    at = lax.div(lax.axis_index("fsdp"), RING)
    return jnp.where(at < 4, at, 11 - at)


def row_block(snake):
    at = lax.rem(snake + 2 * RING, RING)
    return jnp.where(at < 4, at, 11 - at)


def encode_kernel(weights, base, keep, give):
    core = my_core()
    for out, half in ((keep, core), (give, 1 - core)):
        for block in range(HALF // BLOCK):
            at = pl.multiple_of(half * HALF + block * BLOCK, BLOCK)
            outer_grad = base[:, pl.ds(at, BLOCK)] - weights[0, :, pl.ds(at, BLOCK)].astype(jnp.float32)
            largest = jnp.max(jnp.abs(outer_grad), axis=1, keepdims=True)
            block_scale = (largest + epsilon) / code_limit
            code_values = (outer_grad / block_scale).astype(jnp.bfloat16)
            decoded = code_values.astype(jnp.float32) * block_scale
            out[:, block * BLOCK:(block + 1) * BLOCK] = decoded.astype(jnp.bfloat16)


def outer_step(summed, base_rows, moment_rows):
    averaged = summed * 0.25
    fresh_moment = momentum_decay * moment_rows + averaged
    fresh_master = base_rows - outer_rate * (averaged + momentum_decay * fresh_moment)
    return fresh_master, fresh_moment


def half_step_kernel(keep, from_core, from_chip, from_both, base, moment, summed, fresh):
    start = pl.multiple_of(my_core() * HALF, HALF)
    f32 = lambda ref: ref[...].astype(jnp.float32)
    total = (f32(keep) + f32(from_core)) + (f32(from_chip) + f32(from_both))
    summed[...] = total
    master, _ = outer_step(total, base[:, pl.ds(start, HALF)], moment[:, pl.ds(start, HALF)])
    fresh[...] = master.astype(jnp.bfloat16)


def whole_step_kernel(mine, theirs, base, moment, master_out, moment_out):
    core = my_core()
    for summed, half in ((mine, core), (theirs, 1 - core)):
        start = pl.multiple_of(half * HALF, HALF)
        master, fresh = outer_step(summed[...], base[:, pl.ds(start, HALF)], moment[:, pl.ds(start, HALF)])
        master_out[:, pl.ds(start, HALF)] = master
        moment_out[:, pl.ds(start, HALF)] = fresh


def bundle_kernel(*refs):
    *pieces, out = refs
    core, snake, z = my_core(), my_snake(), my_z()
    for step, piece in enumerate(pieces):
        at = jnp.where(core == 0, row_block(snake + step), lax.rem(z + step, RING))
        out[pl.ds(at, 1)] = piece[...][None]


def assemble_kernel(steps, *refs):
    *refs, sems = refs
    n = len(steps)
    mine, theirs, out = refs[:n], refs[n:2 * n], refs[-1]
    core, snake, z = my_core(), my_snake(), my_z()

    def copies(low, high):
        for i, step in enumerate(steps):
            to_z = lax.rem(z + step + RING, RING)
            yield pltpu.make_async_copy(low[i], out.at[:, to_z, :, pl.ds(0, HALF)], sems.at[2 * i])
            yield pltpu.make_async_copy(high[i], out.at[row_block(snake + step), :, :, pl.ds(HALF, HALF)], sems.at[2 * i + 1])

    @pl.when(core == 0)
    def _():
        todo = list(copies(mine, theirs))
        for copy in todo:
            copy.start()
        for copy in todo:
            copy.wait()

    @pl.when(core == 1)
    def _():
        todo = list(copies(theirs, mine))
        for copy in todo:
            copy.start()
        for copy in todo:
            copy.wait()


VMEM = pl.BlockSpec(memory_space=pltpu.VMEM)
ANY = pl.BlockSpec(memory_space=pl.ANY)


def shape(dims, kind):
    return jax.ShapeDtypeStruct(dims, kind)


def hints(moved, scratch):
    return {
        "cost_estimate": pl.CostEstimate(flops=moved, bytes_accessed=moved, transcendentals=0),
        "compiler_params": pltpu.CompilerParams(vmem_limit_bytes=scratch),
    }


def assemble(steps, mine, theirs, out=None):
    given = [*mine, *theirs] + ([] if out is None else [out])
    return pl.pallas_call(
        functools.partial(assemble_kernel, steps),
        out_shape=shape((8, 8, ROWS, 2 * HALF), jnp.bfloat16),
        in_specs=[ANY] * len(given),
        out_specs=ANY,
        scratch_shapes=[pltpu.SemaphoreType.DMA((2 * len(steps),))],
        input_output_aliases={} if out is None else {len(given) - 1: 0},
        **hints(len(steps) << 21, 1 << 20),
        name="assemble",
    )(*given)


def on_device(local_weights, base, moment):
    bf16, f32 = jnp.bfloat16, jnp.float32
    keep, give = pl.pallas_call(
        encode_kernel,
        out_shape=(shape((ROWS, HALF), bf16),) * 2,
        in_specs=[VMEM] * 2, out_specs=(VMEM,) * 2, **hints(1 << 20, 4 << 20), name="encode",
    )(local_weights, base)
    peers = send(give, OTHER_BOTH), send(keep, OTHER_CHIP), send(give, OTHER_CORE)
    summed, fresh = pl.pallas_call(
        half_step_kernel,
        out_shape=(shape((ROWS, HALF), f32), shape((ROWS, HALF), bf16)),
        in_specs=[VMEM] * 6, out_specs=(VMEM,) * 2, **hints(1 << 20, 4 << 20), name="half_step",
    )(keep, peers[2], peers[1], peers[0], base, moment)

    pieces = [fresh] + [send(fresh, first_phase(-step)) for step in range(1, RING)]
    bundle = pl.pallas_call(
        bundle_kernel,
        out_shape=shape((8, ROWS, HALF), bf16),
        in_specs=[VMEM] * 8, out_specs=VMEM, **hints(1 << 20, 4 << 20), name="bundle",
    )(*pieces)

    theirs_summed = send(summed, OTHER_CORE)
    master, fresh_moment = pl.pallas_call(
        whole_step_kernel,
        out_shape=(shape((ROWS, 2 * HALF), f32),) * 2,
        in_specs=[VMEM] * 4, out_specs=(VMEM,) * 2, **hints(1 << 20, 4 << 20), name="whole_step",
    )(summed, theirs_summed, base, moment)

    mine = {0: bundle}
    for step in range(1, 5):
        mine[step] = send(mine[step - 1], second_phase(-1))
        if step < 4:
            mine[-step] = send(mine[1 - step], second_phase(1))
    theirs = {step: send(x, OTHER_CORE) for step, x in mine.items()}
    out = None
    for steps in ((0, 1, -1), (2, -2), (3, -3), (4,)):
        out = assemble(steps, [mine[s] for s in steps], [theirs[s] for s in steps], out)
    return master, fresh_moment, out.reshape(512, 2 * HALF)


def solution(mesh):
    return jax.shard_map(
        on_device,
        mesh=mesh,
        in_specs=(P("island", "fsdp", None), P("fsdp", None), P("fsdp", None)),
        out_specs=(P("fsdp", None), P("fsdp", None), P()),
        check_vma=False,
    )
```

```python
import functools

import jax
import jax.numpy as jnp
from jax import lax
from jax.experimental import pallas as pl
from jax.experimental.pallas import tpu as pltpu
from jax.sharding import PartitionSpec as P

BLOCK = 128

epsilon = 1e-06
code_limit = 31.0
momentum_decay = 0.9
outer_rate = 0.7

AXES = ("island", "fsdp")
RING = 8
HALF = 4096
ROWS = 8


def all_places():
    for x_lo in range(2):
        for core in range(2):
            for x_hi in range(2):
                for y in range(4):
                    for z in range(8):
                        yield x_lo, core, x_hi, y, z


def number(place):
    x_lo, core, x_hi, y, z = place
    return (x_lo * 2 + core) * 64 + (x_hi * 4 + y) * 8 + z


def pairs(target):
    return [(number(p), number(target(*p))) for p in all_places()]


def snake_of(x_hi, y):
    return y if x_hi == 0 else 7 - y


def along_snake(x_lo, core, x_hi, y, z, step):
    at = (snake_of(x_hi, y) + step) % RING
    to_hi, to_y = (0, at) if at < 4 else (1, 7 - at)
    return (x_lo if to_hi == x_hi else 1 - x_lo), core, to_hi, to_y, z


def along_z(x_lo, core, x_hi, y, z, step):
    return x_lo, core, x_hi, y, (z + step) % RING


def first_phase(step):
    return pairs(lambda *p: (along_snake if p[1] == 0 else along_z)(*p, step))


def second_phase(step):
    return pairs(lambda *p: (along_z if p[1] == 0 else along_snake)(*p, step))


OTHER_CORE = pairs(lambda x_lo, core, x_hi, y, z: (x_lo, 1 - core, x_hi, y, z))
OTHER_CHIP = pairs(lambda x_lo, core, x_hi, y, z: (1 - x_lo, core, x_hi, y, z))
OTHER_BOTH = pairs(lambda x_lo, core, x_hi, y, z: (1 - x_lo, 1 - core, x_hi, y, z))


def send(x, to):
    return lax.ppermute(x, AXES, to)


def my_core():
    return lax.rem(lax.axis_index("island"), 2)


def my_z():
    return lax.rem(lax.axis_index("fsdp"), RING)


def my_snake():
    at = lax.div(lax.axis_index("fsdp"), RING)
    return jnp.where(at < 4, at, 11 - at)


def row_block(snake):
    at = lax.rem(snake + 2 * RING, RING)
    return jnp.where(at < 4, at, 11 - at)


def encode_kernel(weights, base, keep, give, base_near):
    core = my_core()
    for out, half in ((keep, core), (give, 1 - core)):
        for block in range(HALF // BLOCK):
            at = pl.multiple_of(half * HALF + block * BLOCK, BLOCK)
            outer_grad = base[:, pl.ds(at, BLOCK)] - weights[0, :, pl.ds(at, BLOCK)].astype(jnp.float32)
            largest = jnp.max(jnp.abs(outer_grad), axis=1, keepdims=True)
            block_scale = (largest + epsilon) / code_limit
            code_values = (outer_grad / block_scale).astype(jnp.bfloat16)
            decoded = code_values.astype(jnp.float32) * block_scale
            out[:, block * BLOCK:(block + 1) * BLOCK] = decoded.astype(jnp.bfloat16)
    base_near[...] = base[...]


def outer_step(summed, base_rows, decayed_rows):
    averaged = summed * 0.25
    fresh_moment = decayed_rows + averaged
    fresh_master = base_rows - outer_rate * (averaged + momentum_decay * fresh_moment)
    return fresh_master, fresh_moment


def half_step_kernel(keep, from_core, from_chip, from_both, base, decayed, summed, fresh):
    start = pl.multiple_of(my_core() * HALF, HALF)
    f32 = lambda ref: ref[...].astype(jnp.float32)
    total = (f32(keep) + f32(from_core)) + (f32(from_chip) + f32(from_both))
    summed[...] = total
    master, _ = outer_step(total, base[:, pl.ds(start, HALF)], decayed[:, pl.ds(start, HALF)])
    fresh[...] = master.astype(jnp.bfloat16)


def whole_step_kernel(mine, theirs, base, decayed, master_out, moment_out, written):
    written[...] = jnp.zeros_like(written)
    core = my_core()
    for summed, half in ((mine, core), (theirs, 1 - core)):
        start = pl.multiple_of(half * HALF, HALF)
        master, fresh = outer_step(summed[...], base[:, pl.ds(start, HALF)], decayed[:, pl.ds(start, HALF)])
        master_out[:, pl.ds(start, HALF)] = master
        moment_out[:, pl.ds(start, HALF)] = fresh


def trio_kernel(before, own, after, trio, duo):
    trio[0], trio[1], trio[2] = before[...], own[...], after[...]
    duo[0], duo[1] = own[...], after[...]


def chunk_kernel(trio, ahead, behind, low, high):
    core, snake, z = my_core(), my_snake(), my_z()
    for pieces, first in ((trio, -1), (ahead, 2), (behind, -3)):
        for i in range(pieces.shape[0]):
            step = first + i
            at = jnp.where(core == 0, row_block(snake + step), lax.rem(z + step + RING, RING))

            @pl.when(at < 4)
            def _():
                low[pl.ds(at, 1)] = pieces[i][None]

            @pl.when(at >= 4)
            def _():
                high[pl.ds(at - 4, 1)] = pieces[i][None]


def pack_kernel(count, *refs):
    for i in range(count):
        refs[-1][i] = refs[i][...]


def assemble_kernel(own, other, *refs):
    *refs, out, written, sems = refs
    core, snake, z = my_core(), my_snake(), my_z()

    def along_z(step, part):
        return out.at[pl.ds(4 * part, 4), lax.rem(z + step + RING, RING), :, pl.ds(0, HALF)]

    def along_snake(step, part):
        return out.at[row_block(snake + step), pl.ds(4 * part, 4), :, pl.ds(HALF, HALF)]

    def copies(at_own, at_other):
        for i, (where, array, place) in enumerate(own + other):
            source = refs[array] if place is None else refs[array].at[place]
            yield pltpu.make_async_copy(source, (at_own if i < len(own) else at_other)(*where), sems.at[i])

    for core_is, places in ((0, (along_z, along_snake)), (1, (along_snake, along_z))):
        @pl.when(core == core_is)
        def _():
            todo = list(copies(*places))
            for copy in todo:
                copy.start()
            for copy in todo:
                copy.wait()

    written[...] = jnp.zeros_like(written)


VMEM = pl.BlockSpec(memory_space=pltpu.VMEM)
ANY = pl.BlockSpec(memory_space=pl.ANY)


def shape(dims, kind):
    return jax.ShapeDtypeStruct(dims, kind)


def hints(moved, scratch):
    return {
        "cost_estimate": pl.CostEstimate(flops=moved, bytes_accessed=moved, transcendentals=0),
        "compiler_params": pltpu.CompilerParams(vmem_limit_bytes=scratch),
    }


def local(kernel, outs, given, scratch=(), grant=4 << 20, name=None, **more):
    return pl.pallas_call(
        kernel,
        out_shape=tuple(shape(*out) for out in outs),
        in_specs=more.pop("in_specs", [VMEM] * len(given)),
        out_specs=(VMEM,) * len(outs),
        scratch_shapes=scratch,
        name=name,
        **hints(1 << 20, grant),
    )(*given)


def assemble(own, other, out=None):
    arrays, placed = [], ([], [])
    for found, given in zip(placed, (own, other)):
        for array, where in given:
            if isinstance(where, list):
                found.extend((place, len(arrays), i) for i, place in enumerate(where))
            else:
                found.append((where, len(arrays), None))
            arrays.append(array)
    chunks = len(placed[0]) + len(placed[1])
    given = arrays + ([] if out is None else [out])
    return pl.pallas_call(
        functools.partial(assemble_kernel, *placed),
        out_shape=(shape((8, 8, ROWS, 2 * HALF), jnp.bfloat16), shape((8, 128), jnp.float32)),
        in_specs=[ANY] * len(given),
        out_specs=(ANY, VMEM),
        scratch_shapes=[pltpu.SemaphoreType.DMA((chunks,))],
        input_output_aliases={} if out is None else {len(given) - 1: 0},
        name="assemble",
        **hints(chunks << 20, 1 << 20),
    )(*given)


def on_device(local_weights, base_in, moment_in):
    bf16, f32 = jnp.bfloat16, jnp.float32
    half, whole = (ROWS, HALF), (ROWS, 2 * HALF)
    keep, give, base = local(
        encode_kernel, [(half, bf16), (half, bf16), (whole, f32)], (local_weights, base_in), name="encode",
    )
    decayed = momentum_decay * moment_in
    from_both, from_chip, from_core = send(give, OTHER_BOTH), send(keep, OTHER_CHIP), send(give, OTHER_CORE)
    summed, fresh = local(
        half_step_kernel, [(half, f32), (half, bf16)],
        (keep, from_core, from_chip, from_both, base, decayed), name="half_step",
    )

    after, before = send(fresh, first_phase(-1)), send(fresh, first_phase(1))
    trio, duo = local(trio_kernel, [((3, *half), bf16), ((2, *half), bf16)], (before, fresh, after), name="trio")
    ahead, behind = send(trio, first_phase(-3)), send(duo, first_phase(3))
    chunks = local(chunk_kernel, [((4, *half), bf16)] * 2, (trio, ahead, behind), name="chunks")

    theirs_summed = send(summed, OTHER_CORE)
    master, fresh_moment, stepped = local(
        whole_step_kernel, [(whole, f32)] * 2 + [((8, 128), f32)], (summed, theirs_summed, base, decayed), name="whole_step",
    )

    mine = {(0, part): chunks[part] for part in range(2)}
    for step in range(1, 5):
        for part in range(2):
            if step < 4 or part == 0:
                mine[step, part] = send(mine[step - 1, part], second_phase(-1))
            if step < 4 or part == 1:
                mine[-step, part] = send(mine[1 - step, part], second_phase(1))
    out, arrived, done = None, [], []
    for step in range(4):
        keys = [k for k in mine if abs(k[0]) == step]
        pack, = local(
            functools.partial(pack_kernel, len(keys)), [((len(keys), 4, *half), bf16)], [mine[k] for k in keys] + done,
            name="pack", grant=1 << 20, in_specs=[VMEM] * len(keys) + [ANY] * len(done),
        )
        out, written = assemble([(pack, keys)], arrived, out)
        done = [written] + ([stepped] if step == 0 else [])
        arrived = [(send(pack, OTHER_CORE), keys)]
    keys = [(4, 0), (-4, 1)]
    *last, _ = lax.optimization_barrier((*(mine[k] for k in keys), written))
    swapped = [(send(x, OTHER_CORE), k) for x, k in zip(last, keys)]
    out, _ = assemble([(mine[k], k) for k in keys], arrived, out)
    out, _ = assemble([], swapped, out)
    return master, fresh_moment, out.reshape(512, 2 * HALF)


def solution(mesh):
    return jax.shard_map(
        on_device,
        mesh=mesh,
        in_specs=(P("island", "fsdp", None), P("fsdp", None), P("fsdp", None)),
        out_specs=(P("fsdp", None), P("fsdp", None), P()),
        check_vma=False,
    )
```

```python
import functools

import jax
import jax.numpy as jnp
from jax import lax
from jax.experimental import pallas as pl
from jax.experimental.pallas import tpu as pltpu
from jax.sharding import PartitionSpec as P

BLOCK = 128

epsilon = 1e-06
code_limit = 31.0
momentum_decay = 0.9
outer_rate = 0.7

AXES = ("island", "fsdp")
HALF = 4096
ROWS = 8


def all_places():
    for x_lo in range(2):
        for core in range(2):
            for x_hi in range(2):
                for y in range(4):
                    for z in range(8):
                        yield x_lo, core, x_hi, y, z


def number(place):
    x_lo, core, x_hi, y, z = place
    return (x_lo * 2 + core) * 64 + (x_hi * 4 + y % 4) * 8 + z


def pairs(target):
    return [(number(p), number(target(*p))) for p in all_places()]


OTHER_CORE = pairs(lambda x_lo, core, x_hi, y, z: (x_lo, 1 - core, x_hi, y, z))
OTHER_CHIP = pairs(lambda x_lo, core, x_hi, y, z: (1 - x_lo, core, x_hi, y, z))
OTHER_BOTH = pairs(lambda x_lo, core, x_hi, y, z: (1 - x_lo, 1 - core, x_hi, y, z))


def z_flipped(bits):
    return pairs(lambda x_lo, core, x_hi, y, z: (x_lo, core, x_hi, y, z ^ bits))


def along_y(sign):
    return pairs(lambda x_lo, core, x_hi, y, z: (x_lo, core, x_hi, y - sign if core == 0 else y + sign, z))


def across(sign):
    return pairs(lambda x_lo, core, x_hi, y, z: (1 - x_lo, core, 1 - x_hi, y if core == 0 else y + sign, z))


def send(x, to):
    return lax.ppermute(x, AXES, to)


def my_core():
    return lax.rem(lax.axis_index("island"), 2)


def my_z():
    return lax.rem(lax.axis_index("fsdp"), 8)


def my_y():
    return lax.rem(lax.div(lax.axis_index("fsdp"), 8), 4)


def my_x_hi():
    return lax.div(lax.axis_index("fsdp"), 32)


def encode_kernel(weights, base, keep, give, base_near):
    core = my_core()
    for out, half in ((keep, core), (give, 1 - core)):
        for block in range(HALF // BLOCK):
            at = pl.multiple_of(half * HALF + block * BLOCK, BLOCK)
            outer_grad = base[:, pl.ds(at, BLOCK)] - weights[0, :, pl.ds(at, BLOCK)].astype(jnp.float32)
            largest = jnp.max(jnp.abs(outer_grad), axis=1, keepdims=True)
            block_scale = (largest + epsilon) / code_limit
            code_values = (outer_grad / block_scale).astype(jnp.bfloat16)
            decoded = code_values.astype(jnp.float32) * block_scale
            out[:, block * BLOCK:(block + 1) * BLOCK] = decoded.astype(jnp.bfloat16)
    base_near[...] = base[...]


def outer_step(summed, base_rows, decayed_rows):
    averaged = summed * 0.25
    fresh_moment = decayed_rows + averaged
    fresh_master = base_rows - outer_rate * (averaged + momentum_decay * fresh_moment)
    return fresh_master, fresh_moment


def half_step_kernel(keep, from_core, from_chip, from_both, base, decayed, summed, fresh):
    start = pl.multiple_of(my_core() * HALF, HALF)
    f32 = lambda ref: ref[...].astype(jnp.float32)
    total = (f32(keep) + f32(from_core)) + (f32(from_chip) + f32(from_both))
    summed[...] = total
    master, _ = outer_step(total, base[:, pl.ds(start, HALF)], decayed[:, pl.ds(start, HALF)])
    fresh[...] = master.astype(jnp.bfloat16)


def whole_step_kernel(mine, theirs, base, decayed, master_out, moment_out, written):
    written[...] = jnp.zeros_like(written)
    core = my_core()
    for summed, half in ((mine, core), (theirs, 1 - core)):
        start = pl.multiple_of(half * HALF, HALF)
        master, fresh = outer_step(summed[...], base[:, pl.ds(start, HALF)], decayed[:, pl.ds(start, HALF)])
        master_out[:, pl.ds(start, HALF)] = master
        moment_out[:, pl.ds(start, HALF)] = fresh


def z_kernel(*refs):
    at, out = lax.rem(my_z(), 4), refs[-1]
    for bits, piece in enumerate(refs[:4]):
        out[pl.ds(at ^ bits, 1)] = piece[...][None]


def join_kernel(mine, theirs, out):
    core = my_core()
    out[:, :, pl.ds(pl.multiple_of(core * HALF, HALF), HALF)] = mine[...]
    out[:, :, pl.ds(pl.multiple_of((1 - core) * HALF, HALF), HALF)] = theirs[...]


def pack_kernel(first, second, *refs):
    refs[-1][0], refs[-1][1] = first[...], second[...]


def append_kernel(first, second, *refs):
    refs[-1][:4], refs[-1][4:] = first[...], second[...]


def cut_kernel(array, *refs):
    refs[-1][...] = array[pl.ds(2 * my_core(), 2)]


def place_of(what, lane, sign):
    x_hi, y = my_x_hi(), my_y()
    to_x, (low, high) = {
        "own": (x_hi, (0, 0)),
        "a": (x_hi, (sign, -sign)),
        "b": (1 - x_hi, (0, -sign)),
        "c": (1 - x_hi, (sign, 2)),
        "cut": (x_hi, (2, 2)),
    }[what]
    return to_x * 4 + lax.rem(y + 4 + jnp.where(lane == 0, low, high), 4)


def assemble_kernel(where, *refs):
    *refs, out, written, sems = refs
    core, half = my_core(), lax.div(my_z(), 4)
    todo = []
    for i, (what, wave, theirs, array, place) in enumerate(where):
        lane = 1 - core if theirs else core
        start = 4 * (half if wave == 0 else 1 - half)
        z = pl.ds(start + 2 * lane, 2) if what == "cut" else pl.ds(start, 4)
        source = refs[array] if place is None else refs[array].at[place if isinstance(place, int) else pl.ds(*place)]
        target = out.at[place_of(what, lane, SIGNS[wave]), z]
        todo.append(pltpu.make_async_copy(source, target, sems.at[i]))
    for copy in todo:
        copy.start()
    for copy in todo:
        copy.wait()
    written[...] = jnp.zeros_like(written)


SIGNS = (1, -1)
VMEM = pl.BlockSpec(memory_space=pltpu.VMEM)
ANY = pl.BlockSpec(memory_space=pl.ANY)


def shape(dims, kind):
    return jax.ShapeDtypeStruct(dims, kind)


def hints(moved, scratch):
    return {
        "cost_estimate": pl.CostEstimate(flops=moved, bytes_accessed=moved, transcendentals=0),
        "compiler_params": pltpu.CompilerParams(vmem_limit_bytes=scratch),
    }


def local(kernel, outs, given, scratch=(), grant=4 << 20, name=None, **more):
    return pl.pallas_call(
        kernel,
        out_shape=tuple(shape(*out) for out in outs),
        in_specs=more.pop("in_specs", [VMEM] * len(given)),
        out_specs=(VMEM,) * len(outs),
        scratch_shapes=scratch,
        name=name,
        **hints(1 << 20, grant),
    )(*given)


def assemble(given, out=None):
    where, size = [], 0
    for number_of, (array, what) in enumerate(given):
        if isinstance(what, tuple):
            what = [(*what, None)]
        where.extend((*item, number_of, place) for *item, place in what)
        size += array.size * 2
    given = [array for array, _ in given] + ([] if out is None else [out])
    return pl.pallas_call(
        functools.partial(assemble_kernel, where),
        out_shape=(shape((8, 8, ROWS, 2 * HALF), jnp.bfloat16), shape((8, 128), jnp.float32)),
        in_specs=[ANY] * len(given),
        out_specs=(ANY, VMEM),
        scratch_shapes=[pltpu.SemaphoreType.DMA((len(where),))],
        input_output_aliases={} if out is None else {len(given) - 1: 0},
        name="assemble",
        **hints(2 * size, 1 << 20),
    )(*given)


def on_device(local_weights, base_in, moment_in):
    bf16, f32 = jnp.bfloat16, jnp.float32
    half, whole = (ROWS, HALF), (ROWS, 2 * HALF)
    keep, give, base = local(
        encode_kernel, [(half, bf16), (half, bf16), (whole, f32)], (local_weights, base_in), name="encode",
    )
    decayed = momentum_decay * moment_in
    from_both, from_chip, from_core = send(give, OTHER_BOTH), send(keep, OTHER_CHIP), send(give, OTHER_CORE)
    summed, fresh = local(
        half_step_kernel, [(half, f32), (half, bf16)],
        (keep, from_core, from_chip, from_both, base, decayed), name="half_step",
    )

    theirs_summed = send(summed, OTHER_CORE)
    master, fresh_moment, stepped = local(
        whole_step_kernel, [(whole, f32)] * 2 + [((8, 128), f32)], (summed, theirs_summed, base, decayed), name="whole_step",
    )

    def small(kernel, dims, given, name, after=()):
        specs = [VMEM] * len(given) + [ANY] * len(after)
        return local(kernel, [(dims, bf16)], [*given, *after], name=name, grant=1 << 20, in_specs=specs)[0]

    far = send(fresh, z_flipped(4))
    bundles = []
    for first, after in ((fresh, (far,)), (far, ())):
        pieces = [first] + [send(first, z_flipped(bits)) for bits in (1, 2, 3)]
        mine = small(z_kernel, (4, *half), pieces, "z_pieces", after)
        bundles.append(small(join_kernel, (4, *whole), (mine, send(mine, OTHER_CORE)), "join"))

    def first_step(wave, bundle):
        return send(bundle, along_y(SIGNS[wave])), send(bundle, across(SIGNS[wave]))

    def second_step(wave, a, b):
        cut = small(cut_kernel, (2, *whole), (a,), "cut")
        return send(b, along_y(SIGNS[wave])), send(cut, along_y(SIGNS[wave]))

    def pair(a, b, after):
        return small(pack_kernel, (2, 4, *whole), (a, b), "pair", after)

    def append(c, d, after):
        return small(append_kernel, (6, *whole), (c, d), "append", after)

    def swap(x):
        return send(x, OTHER_CORE)

    def holds(what, wave, theirs):
        first, second = what
        if second == "cut":
            return [(first, wave, theirs, (0, 4)), (second, wave, theirs, (4, 2))]
        return [(first, wave, theirs, 0), (second, wave, theirs, 1)]

    ab, cd = ("a", "b"), ("c", "cut")
    a_0, b_0 = first_step(0, bundles[0])
    a_1, b_1 = first_step(1, bundles[1])
    a_0, b_0, bundles[1] = lax.optimization_barrier((a_0, b_0, bundles[1]))
    c_0, d_0 = second_step(0, a_0, b_0)
    pair_0 = pair(a_0, b_0, ())
    out, written = assemble([
        (bundles[0], ("own", 0, False)), (bundles[1], ("own", 1, False)), (pair_0, holds(ab, 0, False)),
    ])
    their_pair_0 = swap(pair_0)
    rest_0 = append(c_0, d_0, (written, stepped))
    a_1, b_1, rest_0 = lax.optimization_barrier((a_1, b_1, rest_0))
    c_1, d_1 = second_step(1, a_1, b_1)
    pair_1 = pair(a_1, b_1, ())
    their_pair_1 = swap(pair_1)
    out, written = assemble([
        (their_pair_0, holds(ab, 0, True)), (pair_1, holds(ab, 1, False)), (rest_0, holds(cd, 0, False)),
    ], out)
    their_rest_0 = swap(rest_0)
    rest_1 = append(c_1, d_1, (written,))
    out, _ = assemble([
        (their_rest_0, holds(cd, 0, True)), (their_pair_1, holds(ab, 1, True)), (rest_1, holds(cd, 1, False)),
    ], out)
    out, _ = assemble([(swap(rest_1), holds(cd, 1, True))], out)
    return master, fresh_moment, out.reshape(512, 2 * HALF)


def solution(mesh):
    return jax.shard_map(
        on_device,
        mesh=mesh,
        in_specs=(P("island", "fsdp", None), P("fsdp", None), P("fsdp", None)),
        out_specs=(P("fsdp", None), P("fsdp", None), P()),
        check_vma=False,
    )
```

```python
import functools

import jax
import jax.numpy as jnp
from jax import lax
from jax.experimental import pallas as pl
from jax.experimental.pallas import tpu as pltpu
from jax.sharding import PartitionSpec as P

BLOCK = 128

epsilon = 1e-06
code_limit = 31.0
momentum_decay = 0.9
outer_rate = 0.7

AXES = ("island", "fsdp")
HALF = 4096
ROWS = 8
PARTS = ((0, 3), (3, 3), (6, 2))


def all_places():
    for x_lo in range(2):
        for core in range(2):
            for x_hi in range(2):
                for y in range(4):
                    for z in range(8):
                        yield x_lo, core, x_hi, y, z


def number(place):
    x_lo, core, x_hi, y, z = place
    return (x_lo * 2 + core) * 64 + (x_hi * 4 + y % 4) * 8 + z


def pairs(target):
    return [(number(p), number(target(*p))) for p in all_places()]


OTHER_CORE = pairs(lambda x_lo, core, x_hi, y, z: (x_lo, 1 - core, x_hi, y, z))
OTHER_CHIP = pairs(lambda x_lo, core, x_hi, y, z: (1 - x_lo, core, x_hi, y, z))
OTHER_BOTH = pairs(lambda x_lo, core, x_hi, y, z: (1 - x_lo, 1 - core, x_hi, y, z))


def from_z(step):
    return pairs(lambda x_lo, core, x_hi, y, z: (x_lo, core, x_hi, y, (z - step) % 8))


FROM_PAIR = pairs(lambda x_lo, core, x_hi, y, z: (x_lo, core, x_hi, y, z ^ 1))


def from_y(step):
    return pairs(lambda x_lo, core, x_hi, y, z: (x_lo, core, x_hi, y - step, z))


FROM_X = pairs(lambda x_lo, core, x_hi, y, z: (1 - x_lo, core, 1 - x_hi, y, z))


def send(x, to):
    return lax.ppermute(x, AXES, to)


def my_core():
    return lax.rem(lax.axis_index("island"), 2)


def my_z():
    return lax.rem(lax.axis_index("fsdp"), 8)


def my_y():
    return lax.rem(lax.div(lax.axis_index("fsdp"), 8), 4)


def my_x_hi():
    return lax.div(lax.axis_index("fsdp"), 32)


def encode_kernel(weights, base, keep, give, base_near):
    core = my_core()
    for out, half in ((keep, core), (give, 1 - core)):
        for block in range(HALF // BLOCK):
            at = pl.multiple_of(half * HALF + block * BLOCK, BLOCK)
            outer_grad = base[:, pl.ds(at, BLOCK)] - weights[0, :, pl.ds(at, BLOCK)].astype(jnp.float32)
            largest = jnp.max(jnp.abs(outer_grad), axis=1, keepdims=True)
            block_scale = (largest + epsilon) / code_limit
            code_values = (outer_grad / block_scale).astype(jnp.bfloat16)
            decoded = code_values.astype(jnp.float32) * block_scale
            out[:, block * BLOCK:(block + 1) * BLOCK] = decoded.astype(jnp.bfloat16)
    base_near[...] = base[...]


def outer_step(summed, base_rows, decayed_rows):
    averaged = summed * 0.25
    fresh_moment = decayed_rows + averaged
    fresh_master = base_rows - outer_rate * (averaged + momentum_decay * fresh_moment)
    return fresh_master, fresh_moment


def half_step_kernel(keep, from_core, from_chip, from_both, base, decayed, summed, fresh):
    start = pl.multiple_of(my_core() * HALF, HALF)
    f32 = lambda ref: ref[...].astype(jnp.float32)
    total = (f32(keep) + f32(from_core)) + (f32(from_chip) + f32(from_both))
    summed[...] = total
    master, _ = outer_step(total, base[:, pl.ds(start, HALF)], decayed[:, pl.ds(start, HALF)])
    fresh[...] = master.astype(jnp.bfloat16)


def whole_step_kernel(mine, theirs, base, decayed, master_out, moment_out, written):
    written[...] = jnp.zeros_like(written)
    core = my_core()
    for summed, half in ((mine, core), (theirs, 1 - core)):
        start = pl.multiple_of(half * HALF, HALF)
        master, fresh = outer_step(summed[...], base[:, pl.ds(start, HALF)], decayed[:, pl.ds(start, HALF)])
        master_out[:, pl.ds(start, HALF)] = master
        moment_out[:, pl.ds(start, HALF)] = fresh


def pair_kernel(own, other, out):
    out[0], out[1] = own[...], other[...]


def bundle_kernel(*refs):
    *couples, out = refs
    z = my_z()
    for step, couple in zip((0, 2, 4, 6), couples):
        for i in range(2):
            out[pl.ds(lax.rem((z ^ i) + step, 8), 1)] = couple[i][None]


def pack_kernel(count, *refs):
    for i in range(count):
        refs[-1][i] = refs[i][...]


def cut_kernel(up, down, across, *outs):
    for ref, (start, count), out in zip((up, down, across), PARTS, outs):
        out[...] = ref[start:start + count]


def last_kernel(*refs):
    for ref, (start, count) in zip(refs, PARTS):
        refs[-1][start:start + count] = ref[...]


def assemble_kernel(where, *refs):
    *refs, out, written, sems = refs
    core, todo = my_core(), []
    for i, (array, place, theirs, flip, up) in enumerate(where):
        source = refs[array] if place is None else refs[array].at[place]
        block = (my_x_hi() ^ flip) * 4 + lax.rem(my_y() + up, 4)
        start = pl.multiple_of((1 - core if theirs else core) * HALF, HALF)
        todo.append(pltpu.make_async_copy(source, out.at[block, :, :, pl.ds(start, HALF)], sems.at[i]))
    for copy in todo:
        copy.start()
    for copy in todo:
        copy.wait()
    written[...] = jnp.zeros_like(written)


VMEM = pl.BlockSpec(memory_space=pltpu.VMEM)
ANY = pl.BlockSpec(memory_space=pl.ANY)


def shape(dims, kind):
    return jax.ShapeDtypeStruct(dims, kind)


def hints(moved, scratch):
    return {
        "cost_estimate": pl.CostEstimate(flops=moved, bytes_accessed=moved, transcendentals=0),
        "compiler_params": pltpu.CompilerParams(vmem_limit_bytes=scratch),
    }


def local(kernel, outs, given, scratch=(), grant=4 << 20, name=None, **more):
    return pl.pallas_call(
        kernel,
        out_shape=tuple(shape(*out) for out in outs),
        in_specs=more.pop("in_specs", [VMEM] * len(given)),
        out_specs=(VMEM,) * len(outs),
        scratch_shapes=scratch,
        name=name,
        **hints(1 << 20, grant),
    )(*given)


def assemble(given, out=None):
    where = []
    for array, (_, theirs, places) in enumerate(given):
        packed = isinstance(places, list)
        where.extend((array, i if packed else None, theirs, *at) for i, at in enumerate(places if packed else [places]))
    given = [array for array, _, _ in given] + ([] if out is None else [out])
    return pl.pallas_call(
        functools.partial(assemble_kernel, where),
        out_shape=(shape((8, 8, ROWS, 2 * HALF), jnp.bfloat16), shape((8, 128), jnp.float32)),
        in_specs=[ANY] * len(given),
        out_specs=(ANY, VMEM),
        scratch_shapes=[pltpu.SemaphoreType.DMA((len(where),))],
        input_output_aliases={} if out is None else {len(given) - 1: 0},
        name="assemble",
        **hints(len(where) << 20, 1 << 20),
    )(*given)


def on_device(local_weights, base_in, moment_in):
    bf16, f32 = jnp.bfloat16, jnp.float32
    half, whole = (ROWS, HALF), (ROWS, 2 * HALF)
    keep, give, base = local(
        encode_kernel, [(half, bf16), (half, bf16), (whole, f32)], (local_weights, base_in), name="encode",
    )
    decayed = momentum_decay * moment_in
    from_both, from_chip, from_core = send(give, OTHER_BOTH), send(keep, OTHER_CHIP), send(give, OTHER_CORE)
    summed, fresh = local(
        half_step_kernel, [(half, f32), (half, bf16)],
        (keep, from_core, from_chip, from_both, base, decayed), name="half_step",
    )

    theirs_summed = send(summed, OTHER_CORE)
    master, fresh_moment, stepped = local(
        whole_step_kernel, [(whole, f32)] * 2 + [((8, 128), f32)], (summed, theirs_summed, base, decayed), name="whole_step",
    )

    def swap(x):
        return send(x, OTHER_CORE)

    def pack(arrays, after):
        return local(
            functools.partial(pack_kernel, len(arrays)), [((len(arrays), *bundle.shape), bf16)], [*arrays, *after],
            name="pack", grant=1 << 20, in_specs=[VMEM] * len(arrays) + [ANY] * len(after),
        )[0]

    couple, = local(pair_kernel, [((2, *half), bf16)], (fresh, send(fresh, FROM_PAIR)), name="couple")
    couples = [couple] + [send(couple, from_z(step)) for step in (2, 4, 6)]
    bundle, = local(bundle_kernel, [((8, *half), bf16)], couples, name="bundle")
    up, down, across = send(bundle, from_y(1)), send(bundle, from_y(-1)), send(bundle, FROM_X)
    up_up, down_across, up_across = send(up, from_y(1)), send(across, from_y(-1)), send(up, FROM_X)
    cuts = local(
        cut_kernel, [((count, *half), bf16) for _, count in PARTS], (up_across, down_across, up_up), name="cut",
    )
    parts = [send(x, to) for x, to in zip(cuts, (from_y(1), from_y(-1), FROM_X))]

    first_places, second_places = [(0, 1), (0, 3), (1, 0)], [(0, 2), (1, 3), (1, 1)]
    their_bundle = swap(bundle)
    first = pack((up, down, across), (stepped,))
    their_first = swap(first)
    out, written = assemble([(bundle, False, (0, 0)), (their_bundle, True, (0, 0)), (first, False, first_places)])
    second = pack((up_up, down_across, up_across), (written,))
    their_second = swap(second)
    out, written = assemble(
        [(their_first, True, first_places), (second, False, second_places), (their_second, True, second_places)], out,
    )
    last, = local(
        last_kernel, [((8, *half), bf16)], [*parts, written], name="last", grant=1 << 20, in_specs=[VMEM] * 3 + [ANY],
    )
    out, _ = assemble([(last, False, (1, 2)), (swap(last), True, (1, 2))], out)
    return master, fresh_moment, out.reshape(512, 2 * HALF)


def solution(mesh):
    return jax.shard_map(
        on_device,
        mesh=mesh,
        in_specs=(P("island", "fsdp", None), P("fsdp", None), P("fsdp", None)),
        out_specs=(P("fsdp", None), P("fsdp", None), P()),
        check_vma=False,
    )
```

```python
import functools

import jax
import jax.numpy as jnp
from jax import lax
from jax.experimental import pallas as pl
from jax.experimental.pallas import tpu as pltpu
from jax.sharding import PartitionSpec as P

BLOCK = 128

epsilon = 1e-06
code_limit = 31.0
momentum_decay = 0.9
outer_rate = 0.7

AXES = ("island", "fsdp")
HALF = 4096
ROWS = 8
RING = 8


def all_places():
    for x_lo in range(2):
        for core in range(2):
            for x_hi in range(2):
                for y in range(4):
                    for z in range(8):
                        yield x_lo, core, x_hi, y, z


def number(place):
    x_lo, core, x_hi, y, z = place
    return (x_lo * 2 + core) * 64 + (x_hi * 4 + y % 4) * 8 + z


def pairs(target):
    return [(number(p), number(target(*p))) for p in all_places()]


OTHER_CORE = pairs(lambda x_lo, core, x_hi, y, z: (x_lo, 1 - core, x_hi, y, z))
OTHER_CHIP = pairs(lambda x_lo, core, x_hi, y, z: (1 - x_lo, core, x_hi, y, z))
OTHER_BOTH = pairs(lambda x_lo, core, x_hi, y, z: (1 - x_lo, 1 - core, x_hi, y, z))


def by_core(first, second):
    return pairs(lambda *p: (first if p[1] == 0 else second)(*p))


def across_x(x_lo, core, x_hi, y, z):
    return 1 - x_lo, core, 1 - x_hi, y, z


def along_y(step):
    return lambda x_lo, core, x_hi, y, z: (x_lo, core, x_hi, y + step, z)


def along_z(step):
    return lambda x_lo, core, x_hi, y, z: (x_lo, core, x_hi, y, (z + step) % 8)


def z_neighbour(x_lo, core, x_hi, y, z):
    return x_lo, core, x_hi, y, z ^ 1


def along_snake(step):
    def target(x_lo, core, x_hi, y, z):
        at = ((y if x_hi == 0 else 7 - y) + step) % RING
        to_x, to_y = (0, at) if at < 4 else (1, 7 - at)
        return (x_lo if to_x == x_hi else 1 - x_lo), core, to_x, to_y, z
    return target


def send(x, to):
    return lax.ppermute(x, AXES, to)


def my_core():
    return lax.rem(lax.axis_index("island"), 2)


def my_z():
    return lax.rem(lax.axis_index("fsdp"), 8)


def my_y():
    return lax.rem(lax.div(lax.axis_index("fsdp"), 8), 4)


def snake_block(step):
    at = lax.div(lax.axis_index("fsdp"), 8)
    at = lax.rem(jnp.where(at < 4, at, 11 - at) + step + RING, RING)
    return jnp.where(at < 4, at, 11 - at)


def my_x_hi():
    return lax.div(lax.axis_index("fsdp"), 32)


def encode_kernel(weights, base, keep, give, base_near):
    core = my_core()
    for out, half in ((keep, core), (give, 1 - core)):
        for block in range(HALF // BLOCK):
            at = pl.multiple_of(half * HALF + block * BLOCK, BLOCK)
            outer_grad = base[:, pl.ds(at, BLOCK)] - weights[0, :, pl.ds(at, BLOCK)].astype(jnp.float32)
            largest = jnp.max(jnp.abs(outer_grad), axis=1, keepdims=True)
            block_scale = (largest + epsilon) / code_limit
            code_values = (outer_grad / block_scale).astype(jnp.bfloat16)
            decoded = code_values.astype(jnp.float32) * block_scale
            out[:, block * BLOCK:(block + 1) * BLOCK] = decoded.astype(jnp.bfloat16)
    base_near[...] = base[...]


def outer_step(summed, base_rows, decayed_rows):
    averaged = summed * 0.25
    fresh_moment = decayed_rows + averaged
    fresh_master = base_rows - outer_rate * (averaged + momentum_decay * fresh_moment)
    return fresh_master, fresh_moment


def half_step_kernel(keep, from_core, from_chip, from_both, base, decayed, summed, fresh):
    start = pl.multiple_of(my_core() * HALF, HALF)
    f32 = lambda ref: ref[...].astype(jnp.float32)
    total = (f32(keep) + f32(from_core)) + (f32(from_chip) + f32(from_both))
    summed[...] = total
    master, _ = outer_step(total, base[:, pl.ds(start, HALF)], decayed[:, pl.ds(start, HALF)])
    fresh[...] = master.astype(jnp.bfloat16)


def whole_step_kernel(mine, theirs, base, decayed, master_out, moment_out, written):
    written[...] = jnp.zeros_like(written)
    core = my_core()
    for summed, half in ((mine, core), (theirs, 1 - core)):
        start = pl.multiple_of(half * HALF, HALF)
        master, fresh = outer_step(summed[...], base[:, pl.ds(start, HALF)], decayed[:, pl.ds(start, HALF)])
        master_out[:, pl.ds(start, HALF)] = master
        moment_out[:, pl.ds(start, HALF)] = fresh


def couple_kernel(own, other, *refs):
    refs[-1][0], refs[-1][1] = own[...], other[...]


def bundle_kernel(*refs):
    *couples, out = refs
    core, x_hi, y, z = my_core(), my_x_hi(), my_y(), my_z()
    for step, couple in enumerate(couples):
        for i in range(2):
            at = jnp.where(core == 0, (x_hi ^ i) * 4 + lax.rem(y + step, 4), lax.rem((z ^ i) + 2 * step, 8))
            out[pl.ds(at, 1)] = couple[i][None]


def pack_kernel(count, *refs):
    for i in range(count):
        refs[-1][i] = refs[i][...]


def cut_kernel(ahead, behind, low, high):
    low[...], high[...] = ahead[:4], behind[4:]


def last_kernel(low, high, *refs):
    refs[-1][:4], refs[-1][4:] = low[...], high[...]


def assemble_kernel(own, other, ends, *refs):
    *refs, sems = refs
    written = None if ends else refs.pop()
    *refs, out = refs

    def copies(where, of_core):
        for array, place, step in where:
            source = refs[array] if place is None else refs[array].at[place]
            if of_core == 0:
                yield source, out.at[:, lax.rem(my_z() + step + RING, RING), :, pl.ds(0, HALF)]
            else:
                yield source, out.at[snake_block(step), :, :, pl.ds(HALF, HALF)]

    for core in range(2):
        @pl.when(my_core() == core)
        def _():
            found = [*copies(own, core), *copies(other, 1 - core)]
            todo = [pltpu.make_async_copy(*ends, sems.at[i]) for i, ends in enumerate(found)]
            for copy in todo:
                copy.start()
            for copy in todo:
                copy.wait()

    if written is not None:
        written[...] = jnp.zeros_like(written)


VMEM = pl.BlockSpec(memory_space=pltpu.VMEM)
ANY = pl.BlockSpec(memory_space=pl.ANY)


def shape(dims, kind):
    return jax.ShapeDtypeStruct(dims, kind)


def hints(moved, scratch):
    return {
        "cost_estimate": pl.CostEstimate(flops=moved, bytes_accessed=moved, transcendentals=0),
        "compiler_params": pltpu.CompilerParams(vmem_limit_bytes=scratch),
    }


def local(kernel, outs, given, scratch=(), grant=4 << 20, name=None, **more):
    return pl.pallas_call(
        kernel,
        out_shape=tuple(shape(*out) for out in outs),
        in_specs=more.pop("in_specs", [VMEM] * len(given)),
        out_specs=(VMEM,) * len(outs),
        scratch_shapes=scratch,
        name=name,
        **hints(1 << 20, grant),
    )(*given)


def assemble(own, other, out=None, ends=False):
    arrays, placed = [], ([], [])
    for found, given in zip(placed, (own, other)):
        for array, steps in given:
            packed = isinstance(steps, list)
            found.extend((len(arrays), i if packed else None, step) for i, step in enumerate(steps if packed else [steps]))
            arrays.append(array)
    count = len(placed[0]) + len(placed[1])
    given = arrays + ([] if out is None else [out])
    return pl.pallas_call(
        functools.partial(assemble_kernel, *placed, ends),
        out_shape=(shape((8, 8, ROWS, 2 * HALF), jnp.bfloat16), shape((8, 128), jnp.float32))[:1 if ends else 2],
        in_specs=[ANY] * len(given),
        out_specs=(ANY, VMEM)[:1 if ends else 2],
        scratch_shapes=[pltpu.SemaphoreType.DMA((count,))],
        input_output_aliases={} if out is None else {len(given) - 1: 0},
        name="assemble",
        **hints(count << 20, 1 << 20),
    )(*given)


def on_device(local_weights, base_in, moment_in):
    bf16, f32 = jnp.bfloat16, jnp.float32
    half, whole = (ROWS, HALF), (ROWS, 2 * HALF)
    local_weights, base_in = (pltpu.with_memory_space_constraint(x, pltpu.HBM) for x in (local_weights, base_in))
    keep, give, base = local(
        encode_kernel, [(half, bf16), (half, bf16), (whole, f32)], (local_weights, base_in), name="encode",
    )
    decayed = momentum_decay * moment_in
    from_both, from_chip, from_core = send(give, OTHER_BOTH), send(keep, OTHER_CHIP), send(give, OTHER_CORE)
    summed, fresh = local(
        half_step_kernel, [(half, f32), (half, bf16)],
        (keep, from_core, from_chip, from_both, base, decayed), name="half_step",
    )

    def swap(x):
        return send(x, OTHER_CORE)

    def pack(arrays, after):
        return local(
            functools.partial(pack_kernel, len(arrays)), [((len(arrays), *bundle.shape), bf16)], [*arrays, *after],
            name="pack", grant=1 << 20, in_specs=[VMEM] * len(arrays) + [ANY] * len(after),
        )[0]

    other = send(fresh, by_core(across_x, z_neighbour))
    theirs_summed = send(summed, OTHER_CORE)
    master, fresh_moment, stepped = local(
        whole_step_kernel, [(whole, f32)] * 2 + [((8, 128), f32)], (summed, theirs_summed, base, decayed), name="whole_step",
    )
    couple, = local(
        couple_kernel, [((2, *half), bf16)], (fresh, other, stepped), name="couple", in_specs=[VMEM] * 2 + [ANY],
    )
    couples = [couple] + [send(couple, by_core(along_y(-step), along_z(-2 * step))) for step in (1, 2, 3)]
    bundle, = local(bundle_kernel, [((8, *half), bf16)], couples, name="bundle")

    ahead, behind = by_core(along_z(-1), along_snake(-1)), by_core(along_z(1), along_snake(1))
    got = {0: bundle}
    for step in (1, 2, 3):
        got[step], got[-step] = send(got[step - 1], ahead), send(got[1 - step], behind)
    low, high = local(cut_kernel, [((4, *half), bf16)] * 2, (got[3], got[-3]), name="cut")
    low, high = send(low, ahead), send(high, behind)

    out, theirs, after = None, [], ()
    for steps in ([0, 1, -1], [2, -2], [3, -3]):
        packed = pack([got[step] for step in steps], after)
        out, written = assemble([(packed, steps)], theirs, out)
        theirs, after = [(swap(packed), steps)], (written,)
    out, written = assemble([], theirs, out)
    last, = local(
        last_kernel, [((8, *half), bf16)], (low, high, written), name="last", grant=1 << 20, in_specs=[VMEM] * 2 + [ANY],
    )
    their_last = swap(last)
    out, = assemble([(last, 4)], [], out, ends=True)
    out, = assemble([], [(their_last, 4)], out, ends=True)
    return master, fresh_moment, out.reshape(512, 2 * HALF)


def solution(mesh):
    return jax.shard_map(
        on_device,
        mesh=mesh,
        in_specs=(P("island", "fsdp", None), P("fsdp", None), P("fsdp", None)),
        out_specs=(P("fsdp", None), P("fsdp", None), P()),
        check_vma=False,
    )
```

```python
import functools

import jax
import jax.numpy as jnp
from jax import lax
from jax.experimental import pallas as pl
from jax.experimental.pallas import tpu as pltpu
from jax.sharding import PartitionSpec as P

BLOCK = 128

epsilon = 1e-06
code_limit = 31.0
momentum_decay = 0.9
outer_rate = 0.7

AXES = ("island", "fsdp")
HALF = 4096
ROWS = 8
RING = 8
SPLIT = 5


def all_places():
    for x_lo in range(2):
        for core in range(2):
            for x_hi in range(2):
                for y in range(4):
                    for z in range(8):
                        yield x_lo, core, x_hi, y, z


def number(place):
    x_lo, core, x_hi, y, z = place
    return (x_lo * 2 + core) * 64 + (x_hi * 4 + y % 4) * 8 + z


def pairs(target):
    return [(number(p), number(target(*p))) for p in all_places()]


OTHER_CORE = pairs(lambda x_lo, core, x_hi, y, z: (x_lo, 1 - core, x_hi, y, z))
OTHER_CHIP = pairs(lambda x_lo, core, x_hi, y, z: (1 - x_lo, core, x_hi, y, z))
OTHER_BOTH = pairs(lambda x_lo, core, x_hi, y, z: (1 - x_lo, 1 - core, x_hi, y, z))


def by_core(first, second):
    return pairs(lambda *p: (first if p[1] == 0 else second)(*p))


def across_x(x_lo, core, x_hi, y, z):
    return 1 - x_lo, core, 1 - x_hi, y, z


def along_y(step):
    return lambda x_lo, core, x_hi, y, z: (x_lo, core, x_hi, y + step, z)


def along_z(step):
    return lambda x_lo, core, x_hi, y, z: (x_lo, core, x_hi, y, (z + step) % 8)


def z_neighbour(x_lo, core, x_hi, y, z):
    return x_lo, core, x_hi, y, z ^ 1


def along_snake(step):
    def target(x_lo, core, x_hi, y, z):
        at = ((y if x_hi == 0 else 7 - y) + step) % RING
        to_x, to_y = (0, at) if at < 4 else (1, 7 - at)
        return (x_lo if to_x == x_hi else 1 - x_lo), core, to_x, to_y, z
    return target


def send(x, to):
    return lax.ppermute(x, AXES, to)


def my_core():
    return lax.rem(lax.axis_index("island"), 2)


def my_z():
    return lax.rem(lax.axis_index("fsdp"), 8)


def my_y():
    return lax.rem(lax.div(lax.axis_index("fsdp"), 8), 4)


def snake_block(step):
    at = lax.div(lax.axis_index("fsdp"), 8)
    at = lax.rem(jnp.where(at < 4, at, 11 - at) + step + RING, RING)
    return jnp.where(at < 4, at, 11 - at)


def my_x_hi():
    return lax.div(lax.axis_index("fsdp"), 32)


def encode_kernel(weights, base, keep, give, base_near):
    core = my_core()
    for out, half in ((keep, core), (give, 1 - core)):
        for block in range(HALF // BLOCK):
            at = pl.multiple_of(half * HALF + block * BLOCK, BLOCK)
            outer_grad = base[:, pl.ds(at, BLOCK)] - weights[0, :, pl.ds(at, BLOCK)].astype(jnp.float32)
            largest = jnp.max(jnp.abs(outer_grad), axis=1, keepdims=True)
            block_scale = (largest + epsilon) / code_limit
            code_values = (outer_grad / block_scale).astype(jnp.bfloat16)
            decoded = code_values.astype(jnp.float32) * block_scale
            out[:, block * BLOCK:(block + 1) * BLOCK] = decoded.astype(jnp.bfloat16)
    base_near[...] = base[...]


def outer_step(summed, base_rows, decayed_rows):
    averaged = summed * 0.25
    fresh_moment = decayed_rows + averaged
    fresh_master = base_rows - outer_rate * (averaged + momentum_decay * fresh_moment)
    return fresh_master, fresh_moment


def half_step_kernel(keep, from_core, from_chip, from_both, base, decayed, summed, fresh):
    start = pl.multiple_of(my_core() * HALF, HALF)
    f32 = lambda ref: ref[...].astype(jnp.float32)
    total = (f32(keep) + f32(from_core)) + (f32(from_chip) + f32(from_both))
    summed[...] = total
    master, _ = outer_step(total, base[:, pl.ds(start, HALF)], decayed[:, pl.ds(start, HALF)])
    fresh[...] = master.astype(jnp.bfloat16)


def whole_step_kernel(mine, theirs, base, decayed, master_out, moment_out, written):
    written[...] = jnp.zeros_like(written)
    core = my_core()
    for summed, half in ((mine, core), (theirs, 1 - core)):
        start = pl.multiple_of(half * HALF, HALF)
        master, fresh = outer_step(summed[...], base[:, pl.ds(start, HALF)], decayed[:, pl.ds(start, HALF)])
        master_out[:, pl.ds(start, HALF)] = master
        moment_out[:, pl.ds(start, HALF)] = fresh


def couple_kernel(own, other, *refs):
    refs[-1][0], refs[-1][1] = own[...], other[...]


def bundle_kernel(*refs):
    *couples, out = refs
    core, x_hi, y, z = my_core(), my_x_hi(), my_y(), my_z()
    for step, couple in zip((0, 2, 1, 3), couples):
        for i in range(2):
            at = jnp.where(core == 0, (x_hi ^ i) * 4 + lax.rem(y + step, 4), lax.rem((z ^ i) + 2 * step, 8))
            out[pl.ds(at, 1)] = couple[i][None]


def pack_kernel(count, *refs):
    for i in range(count):
        refs[-1][i] = refs[i][...]


def cut_kernel(start, bundle, part):
    part[...] = bundle[start:start + part.shape[0]]


def last_kernel(low, high, *refs):
    refs[-1][:SPLIT], refs[-1][SPLIT:] = low[...], high[...]


def assemble_kernel(own, other, ends, *refs):
    *refs, sems = refs
    written = None if ends else refs.pop()
    *refs, out = refs

    def copies(where, of_core):
        for array, place, step in where:
            source = refs[array] if place is None else refs[array].at[place]
            if of_core == 0:
                yield source, out.at[:, lax.rem(my_z() + step + RING, RING), :, pl.ds(0, HALF)]
            else:
                yield source, out.at[snake_block(step), :, :, pl.ds(HALF, HALF)]

    for core in range(2):
        @pl.when(my_core() == core)
        def _():
            found = [*copies(own, core), *copies(other, 1 - core)]
            todo = [pltpu.make_async_copy(*ends, sems.at[i]) for i, ends in enumerate(found)]
            for copy in todo:
                copy.start()
            for copy in todo:
                copy.wait()

    if written is not None:
        written[...] = jnp.zeros_like(written)


VMEM = pl.BlockSpec(memory_space=pltpu.VMEM)
ANY = pl.BlockSpec(memory_space=pl.ANY)


def shape(dims, kind):
    return jax.ShapeDtypeStruct(dims, kind)


def hints(moved, scratch):
    return {
        "cost_estimate": pl.CostEstimate(flops=moved, bytes_accessed=moved, transcendentals=0),
        "compiler_params": pltpu.CompilerParams(vmem_limit_bytes=scratch),
    }


def local(kernel, outs, given, scratch=(), grant=4 << 20, name=None, **more):
    return pl.pallas_call(
        kernel,
        out_shape=tuple(shape(*out) for out in outs),
        in_specs=more.pop("in_specs", [VMEM] * len(given)),
        out_specs=(VMEM,) * len(outs),
        scratch_shapes=scratch,
        name=name,
        **hints(1 << 20, grant),
    )(*given)


def assemble(own, other, out=None, ends=False):
    arrays, placed = [], ([], [])
    for found, given in zip(placed, (own, other)):
        for array, steps in given:
            packed = isinstance(steps, list)
            found.extend((len(arrays), i if packed else None, step) for i, step in enumerate(steps if packed else [steps]))
            arrays.append(array)
    count = len(placed[0]) + len(placed[1])
    given = arrays + ([] if out is None else [out])
    return pl.pallas_call(
        functools.partial(assemble_kernel, *placed, ends),
        out_shape=(shape((8, 8, ROWS, 2 * HALF), jnp.bfloat16), shape((8, 128), jnp.float32))[:1 if ends else 2],
        in_specs=[ANY] * len(given),
        out_specs=(ANY, VMEM)[:1 if ends else 2],
        scratch_shapes=[pltpu.SemaphoreType.DMA((count,))],
        input_output_aliases={} if out is None else {len(given) - 1: 0},
        name="assemble",
        **hints(count << 20, 1 << 20),
    )(*given)


def on_device(local_weights, base_in, moment_in):
    bf16, f32 = jnp.bfloat16, jnp.float32
    half, whole = (ROWS, HALF), (ROWS, 2 * HALF)
    local_weights, base_in = (pltpu.with_memory_space_constraint(x, pltpu.HBM) for x in (local_weights, base_in))
    keep, give, base = local(
        encode_kernel, [(half, bf16), (half, bf16), (whole, f32)], (local_weights, base_in), name="encode",
    )
    decayed = momentum_decay * moment_in
    from_both, from_chip, from_core = send(give, OTHER_BOTH), send(keep, OTHER_CHIP), send(give, OTHER_CORE)
    summed, fresh = local(
        half_step_kernel, [(half, f32), (half, bf16)],
        (keep, from_core, from_chip, from_both, base, decayed), name="half_step",
    )

    def swap(x):
        return send(x, OTHER_CORE)

    def pack(arrays, after):
        return local(
            functools.partial(pack_kernel, len(arrays)), [((len(arrays), *bundle.shape), bf16)], [*arrays, *after],
            name="pack", grant=1 << 20, in_specs=[VMEM] * len(arrays) + [ANY] * len(after),
        )[0]

    other = send(fresh, by_core(across_x, z_neighbour))
    theirs_summed = send(summed, OTHER_CORE)
    master, fresh_moment, stepped = local(
        whole_step_kernel, [(whole, f32)] * 2 + [((8, 128), f32)], (summed, theirs_summed, base, decayed), name="whole_step",
    )
    couple, = local(
        couple_kernel, [((2, *half), bf16)], (fresh, other, stepped), name="couple", in_specs=[VMEM] * 2 + [ANY],
    )
    couples = [couple] + [send(couple, by_core(along_y(-step), along_z(-2 * step))) for step in (2, 1, 3)]
    bundle, = local(bundle_kernel, [((8, *half), bf16)], couples, name="bundle")

    ahead, behind = by_core(along_z(-1), along_snake(-1)), by_core(along_z(1), along_snake(1))
    got = {0: bundle}
    for step in (1, 2, 3):
        got[step], got[-step] = send(got[step - 1], ahead), send(got[1 - step], behind)
    def cut(bundle, start, count):
        return local(functools.partial(cut_kernel, start), [((count, *half), bf16)], (bundle,), name="cut", grant=1 << 20)[0]

    low, high = send(cut(got[3], 0, SPLIT), ahead), send(cut(got[-3], SPLIT, 8 - SPLIT), behind)

    out, theirs, after = None, [], ()
    for steps in ([0, 1, -1], [2, -2], [3, -3]):
        packed = pack([got[step] for step in steps], after)
        out, written = assemble([(packed, steps)], theirs, out)
        theirs, after = [(swap(packed), steps)], (written,)
    out, written = assemble([], theirs, out)
    last, = local(
        last_kernel, [((8, *half), bf16)], (low, high, written), name="last", grant=1 << 20, in_specs=[VMEM] * 2 + [ANY],
    )
    their_last = swap(last)
    out, = assemble([(last, 4)], [], out, ends=True)
    out, = assemble([], [(their_last, 4)], out, ends=True)
    return master, fresh_moment, out.reshape(512, 2 * HALF)


def solution(mesh):
    return jax.shard_map(
        on_device,
        mesh=mesh,
        in_specs=(P("island", "fsdp", None), P("fsdp", None), P("fsdp", None)),
        out_specs=(P("fsdp", None), P("fsdp", None), P()),
        check_vma=False,
    )
```

```python
import functools

import jax
import jax.numpy as jnp
from jax import lax
from jax.experimental import pallas as pl
from jax.experimental.pallas import tpu as pltpu
from jax.sharding import PartitionSpec as P

BLOCK = 128

epsilon = 1e-06
code_limit = 31.0
momentum_decay = 0.9
outer_rate = 0.7

AXES = ("island", "fsdp")
HALF = 4096
ROWS = 8
RING = 8
SPLIT = 5


def all_places():
    for x_lo in range(2):
        for core in range(2):
            for x_hi in range(2):
                for y in range(4):
                    for z in range(8):
                        yield x_lo, core, x_hi, y, z


def number(place):
    x_lo, core, x_hi, y, z = place
    return (x_lo * 2 + core) * 64 + (x_hi * 4 + y % 4) * 8 + z


def pairs(target):
    return [(number(p), number(target(*p))) for p in all_places()]


OTHER_CORE = pairs(lambda x_lo, core, x_hi, y, z: (x_lo, 1 - core, x_hi, y, z))
OTHER_CHIP = pairs(lambda x_lo, core, x_hi, y, z: (1 - x_lo, core, x_hi, y, z))
OTHER_BOTH = pairs(lambda x_lo, core, x_hi, y, z: (1 - x_lo, 1 - core, x_hi, y, z))


def by_core(first, second):
    return pairs(lambda *p: (first if p[1] == 0 else second)(*p))


def across_x(x_lo, core, x_hi, y, z):
    return 1 - x_lo, core, 1 - x_hi, y, z


def along_y(step):
    return lambda x_lo, core, x_hi, y, z: (x_lo, core, x_hi, y + step, z)


def along_z(step):
    return lambda x_lo, core, x_hi, y, z: (x_lo, core, x_hi, y, (z + step) % 8)


def z_neighbour(x_lo, core, x_hi, y, z):
    return x_lo, core, x_hi, y, z ^ 1


def along_snake(step):
    def target(x_lo, core, x_hi, y, z):
        at = ((y if x_hi == 0 else 7 - y) + step) % RING
        to_x, to_y = (0, at) if at < 4 else (1, 7 - at)
        return (x_lo if to_x == x_hi else 1 - x_lo), core, to_x, to_y, z
    return target


def send(x, to):
    return lax.ppermute(x, AXES, to)


def my_core():
    return lax.rem(lax.axis_index("island"), 2)


def my_z():
    return lax.rem(lax.axis_index("fsdp"), 8)


def my_y():
    return lax.rem(lax.div(lax.axis_index("fsdp"), 8), 4)


def snake_block(step):
    at = lax.div(lax.axis_index("fsdp"), 8)
    at = lax.rem(jnp.where(at < 4, at, 11 - at) + step + RING, RING)
    return jnp.where(at < 4, at, 11 - at)


def my_x_hi():
    return lax.div(lax.axis_index("fsdp"), 32)


def encode_kernel(weights, base, keep, give, base_near):
    core = my_core()
    for out, half in ((keep, core), (give, 1 - core)):
        for block in range(HALF // BLOCK):
            at = pl.multiple_of(half * HALF + block * BLOCK, BLOCK)
            outer_grad = base[:, pl.ds(at, BLOCK)] - weights[0, :, pl.ds(at, BLOCK)].astype(jnp.float32)
            largest = jnp.max(jnp.abs(outer_grad), axis=1, keepdims=True)
            block_scale = (largest + epsilon) / code_limit
            code_values = (outer_grad / block_scale).astype(jnp.bfloat16)
            decoded = code_values.astype(jnp.float32) * block_scale
            out[:, block * BLOCK:(block + 1) * BLOCK] = decoded.astype(jnp.bfloat16)
    base_near[...] = base[...]


def outer_step(summed, base_rows, decayed_rows):
    averaged = summed * 0.25
    fresh_moment = decayed_rows + averaged
    fresh_master = base_rows - outer_rate * (averaged + momentum_decay * fresh_moment)
    return fresh_master, fresh_moment


def half_step_kernel(keep, from_core, from_chip, from_both, base, decayed, summed, fresh):
    start = pl.multiple_of(my_core() * HALF, HALF)
    f32 = lambda ref: ref[...].astype(jnp.float32)
    total = (f32(keep) + f32(from_core)) + (f32(from_chip) + f32(from_both))
    summed[...] = total
    master, _ = outer_step(total, base[:, pl.ds(start, HALF)], decayed[:, pl.ds(start, HALF)])
    fresh[...] = master.astype(jnp.bfloat16)


def whole_step_kernel(mine, theirs, base, decayed, master_out, moment_out, written):
    written[...] = jnp.zeros_like(written)
    core = my_core()
    for summed, half in ((mine, core), (theirs, 1 - core)):
        start = pl.multiple_of(half * HALF, HALF)
        master, fresh = outer_step(summed[...], base[:, pl.ds(start, HALF)], decayed[:, pl.ds(start, HALF)])
        master_out[:, pl.ds(start, HALF)] = master
        moment_out[:, pl.ds(start, HALF)] = fresh


def couple_kernel(own, other, *refs):
    refs[-1][0], refs[-1][1] = own[...], other[...]


def bundle_kernel(*refs):
    *couples, out = refs
    core, x_hi, y, z = my_core(), my_x_hi(), my_y(), my_z()
    for step, couple in zip((0, 2, 1, 3), couples):
        for i in range(2):
            at = jnp.where(core == 0, (x_hi ^ i) * 4 + lax.rem(y + step, 4), lax.rem((z ^ i) + 2 * step, 8))
            out[pl.ds(at, 1)] = couple[i][None]


def pack_kernel(count, *refs):
    for i in range(count):
        refs[-1][i] = refs[i][...]


def cut_kernel(start, bundle, part):
    part[...] = bundle[start:start + part.shape[0]]


def last_kernel(low, high, *refs):
    refs[-1][:SPLIT], refs[-1][SPLIT:] = low[...], high[...]


def assemble_kernel(own, other, ends, *refs):
    *refs, sems = refs
    written = None if ends else refs.pop()
    *refs, out = refs

    def copies(where, of_core):
        for array, place, step in where:
            source = refs[array] if place is None else refs[array].at[place]
            if of_core == 0:
                yield source, out.at[:, lax.rem(my_z() + step + RING, RING), :, pl.ds(0, HALF)]
            else:
                yield source, out.at[snake_block(step), :, :, pl.ds(HALF, HALF)]

    for core in range(2):
        @pl.when(my_core() == core)
        def _():
            found = [*copies(own, core), *copies(other, 1 - core)]
            todo = [pltpu.make_async_copy(*ends, sems.at[i]) for i, ends in enumerate(found)]
            for copy in todo:
                copy.start()
            for copy in todo:
                copy.wait()

    if written is not None:
        written[...] = jnp.zeros_like(written)


VMEM = pl.BlockSpec(memory_space=pltpu.VMEM)
ANY = pl.BlockSpec(memory_space=pl.ANY)


def shape(dims, kind):
    return jax.ShapeDtypeStruct(dims, kind)


def hints(moved, scratch):
    return {
        "cost_estimate": pl.CostEstimate(flops=moved, bytes_accessed=moved, transcendentals=0),
        "compiler_params": pltpu.CompilerParams(vmem_limit_bytes=scratch),
    }


def local(kernel, outs, given, scratch=(), grant=4 << 20, name=None, **more):
    return pl.pallas_call(
        kernel,
        out_shape=tuple(shape(*out) for out in outs),
        in_specs=more.pop("in_specs", [VMEM] * len(given)),
        out_specs=(VMEM,) * len(outs),
        scratch_shapes=scratch,
        name=name,
        **hints(1 << 20, grant),
    )(*given)


def assemble(own, other, out=None, ends=False):
    arrays, placed = [], ([], [])
    for found, given in zip(placed, (own, other)):
        for array, steps in given:
            packed = isinstance(steps, list)
            found.extend((len(arrays), i if packed else None, step) for i, step in enumerate(steps if packed else [steps]))
            arrays.append(array)
    count = len(placed[0]) + len(placed[1])
    given = arrays + ([] if out is None else [out])
    return pl.pallas_call(
        functools.partial(assemble_kernel, *placed, ends),
        out_shape=(shape((8, 8, ROWS, 2 * HALF), jnp.bfloat16), shape((8, 128), jnp.float32))[:1 if ends else 2],
        in_specs=[ANY] * len(given),
        out_specs=(ANY, VMEM)[:1 if ends else 2],
        scratch_shapes=[pltpu.SemaphoreType.DMA((count,))],
        input_output_aliases={} if out is None else {len(given) - 1: 0},
        name="assemble",
        **hints(count << 20, 1 << 20),
    )(*given)


def on_device(local_weights, base_in, moment_in):
    bf16, f32 = jnp.bfloat16, jnp.float32
    half, whole = (ROWS, HALF), (ROWS, 2 * HALF)
    local_weights, base_in = (pltpu.with_memory_space_constraint(x, pltpu.HBM) for x in (local_weights, base_in))
    keep, give, base = local(
        encode_kernel, [(half, bf16), (half, bf16), (whole, f32)], (local_weights, base_in), name="encode",
    )
    decayed = momentum_decay * moment_in
    from_both, from_chip, from_core = send(give, OTHER_BOTH), send(keep, OTHER_CHIP), send(give, OTHER_CORE)
    summed, fresh = local(
        half_step_kernel, [(half, f32), (half, bf16)],
        (keep, from_core, from_chip, from_both, base, decayed), name="half_step",
    )

    def swap(x):
        return send(x, OTHER_CORE)

    def pack(arrays, after):
        return local(
            functools.partial(pack_kernel, len(arrays)), [((len(arrays), *bundle.shape), bf16)], [*arrays, *after],
            name="pack", grant=1 << 20, in_specs=[VMEM] * len(arrays) + [ANY] * len(after),
        )[0]

    other = send(fresh, by_core(across_x, z_neighbour))
    theirs_summed = send(summed, OTHER_CORE)
    master, fresh_moment, stepped = local(
        whole_step_kernel, [(whole, f32)] * 2 + [((8, 128), f32)], (summed, theirs_summed, base, decayed), name="whole_step",
    )
    couple, = local(
        couple_kernel, [((2, *half), bf16)], (fresh, other, stepped), name="couple", in_specs=[VMEM] * 2 + [ANY],
    )
    couples = [couple] + [send(couple, by_core(along_y(-step), along_z(-2 * step))) for step in (2, 1, 3)]
    bundle, = local(bundle_kernel, [((8, *half), bf16)], couples, name="bundle")

    ahead, behind = by_core(along_z(-1), along_snake(-1)), by_core(along_z(1), along_snake(1))
    got = {0: bundle}
    for step in (1, 2, 3):
        got[step], got[-step] = send(got[step - 1], ahead), send(got[1 - step], behind)
    def cut(bundle, start, count):
        return local(functools.partial(cut_kernel, start), [((count, *half), bf16)], (bundle,), name="cut", grant=1 << 20)[0]

    low, high = send(cut(got[3], 0, SPLIT), ahead), send(cut(got[-3], SPLIT, 8 - SPLIT), behind)

    out, theirs, after = None, [], ()
    for steps in ([0, 1, -1], [2, -2, 3, -3]):
        packed = pack([got[step] for step in steps], after)
        out, written = assemble([(packed, steps)], theirs, out)
        theirs, after = [(swap(packed), steps)], (written,)
    out, written = assemble([], theirs, out)
    last, = local(
        last_kernel, [((8, *half), bf16)], (low, high, written), name="last", grant=1 << 20, in_specs=[VMEM] * 2 + [ANY],
    )
    their_last = swap(last)
    out, = assemble([(last, 4)], [], out, ends=True)
    out, = assemble([], [(their_last, 4)], out, ends=True)
    return master, fresh_moment, out.reshape(512, 2 * HALF)


def solution(mesh):
    return jax.shard_map(
        on_device,
        mesh=mesh,
        in_specs=(P("island", "fsdp", None), P("fsdp", None), P("fsdp", None)),
        out_specs=(P("fsdp", None), P("fsdp", None), P()),
        check_vma=False,
    )
```
